512 devices in a mesh: seq: 128 (over y, z, core), tp: 4 (over x).
Axes of the slice: x: 4, y: 4, z: 16, core: 2. Of those that a mesh axis runs over, the one named last changes fastest.
Arguments:
- queries: float32 [16384, 2048], P('seq', 'tp'), may hold values from -6 to 6
- keys: float32 [16384, 2048], P('seq', 'tp'), may hold values from -6 to 6
- values: float32 [16384, 2048], P('seq', 'tp'), may hold values from -6 to 6
- out_weight: float32 [2048, 4096], P('seq', 'tp'), may hold values from -0.125 to 0.125
Outputs:
- mixed: float32 [16384, 4096], P('seq', 'tp')
The draws below stay inside these ranges and needn't reach their ends.
All inputs are finite; a program needn't handle non-finite values.
Results may differ from the reference program's by a relative error of at most 0.0003.
Values sent between devices are 32-bit elements; how exact they have to be, the bound alone decides.
A program may use at most 128 MiB of HBM per device.

```python
import math
import jax
import jax.numpy as jnp
from jax import lax

D = 4096
HEADS = 16
DH = 128
TOK_DEV = 128
TOKENS = 16384
HD = 2048


def draw_values(key, part):
    noise_key = jax.random.fold_in(key, 11)
    offset_key = jax.random.fold_in(key, 12)
    block_count = TOKENS // TOK_DEV
    noise_part = jax.random.normal(noise_key, (TOKENS, HEADS * DH), jnp.float32)
    offsets = jax.random.normal(offset_key, (block_count, HEADS * DH), jnp.float32)
    spread = jnp.repeat(offsets, TOK_DEV, axis=0)
    return jnp.clip(noise_part + spread, -6.0, 6.0)


def level_of(key, extent, shards, least, top_value):
    def one(dim, blocks):
        draws = jax.random.uniform(jax.random.fold_in(jax.random.fold_in(key, 6), dim), (blocks,), jnp.float32, least / len(shards), top_value / len(shards))
        return jnp.repeat(jnp.exp(draws), extent[dim] // blocks).reshape((-1,) + (1,) * (len(extent) - dim - 1))

    loudness = one(*shards[0])
    for cut in shards[1:]:
        loudness = loudness * one(*cut)
    return loudness


def bell_draw(rng, dims, width, bound, pieces=(), dtype=jnp.bfloat16):
    gain = level_of(rng, dims, pieces, -0.22, 0.18) if pieces else 1.0
    entries = jax.random.normal(rng, dims, jnp.float32) * width * gain
    return jnp.minimum(jnp.maximum(entries, -bound), bound).astype(dtype)


def setup_inputs(seed: int = 0) -> dict:
    key_list = jax.random.split(jax.random.key(seed), 5)
    return {
        "queries": bell_draw(key_list[0], (TOKENS, HD), 1.0, 6.0, ((0, 128), (1, 4)), jnp.float32),
        "keys": bell_draw(key_list[1], (TOKENS, HD), 1.0, 6.0, ((0, 128), (1, 4)), jnp.float32),
        "values": draw_values(jax.random.fold_in(key_list[4], 71), 0),
        "out_weight": bell_draw(key_list[3], (HD, D), HD ** -0.5, 0.125, ((0, 128), (1, 4)), jnp.float32),
    }


def features(inputs):
    return jnp.where(inputs > 0, inputs + 1.0, jnp.exp(jnp.minimum(inputs, 0.0)))


def reference(queries, keys, values, out_weight):
    highest = lax.Precision.HIGHEST
    block_rows = math.gcd(TOKENS, 512)
    block_count = TOKENS // block_rows
    phi_queries = features(queries).reshape(block_count, block_rows, HEADS, DH)
    phi_keys = features(keys).reshape(block_count, block_rows, HEADS, DH)
    value_heads = values.reshape(block_count, block_rows, HEADS, DH)
    causal_mask = jnp.arange(block_rows)[:, None] >= jnp.arange(block_rows)[None, :]

    def advance(carried, blocks):
        memory_state, key_total = carried
        query_block, key_block, value_block = blocks
        scores = jnp.einsum("thd,shd->hts", query_block, key_block, precision=highest)
        scores = jnp.where(causal_mask[None], scores, 0.0)
        numerator = jnp.einsum("hts,shd->thd", scores, value_block, precision=highest)
        numerator = numerator + jnp.einsum("thd,hde->the", query_block, memory_state, precision=highest)
        denominator = jnp.sum(scores, axis=2).T + jnp.einsum("thd,hd->th", query_block, key_total, precision=highest)
        attended = numerator / denominator[:, :, None]
        memory_state = memory_state + jnp.einsum("shd,she->hde", key_block, value_block, precision=highest)
        key_total = key_total + jnp.sum(key_block, axis=0)
        return (memory_state, key_total), attended.reshape(block_rows, HEADS * DH)

    initial = (jnp.zeros((HEADS, DH, DH), jnp.float32), jnp.zeros((HEADS, DH), jnp.float32))
    _, attended = lax.scan(advance, initial, (phi_queries, phi_keys, value_heads))
    attended = attended.reshape(TOKENS, HEADS * DH)
    return jnp.dot(attended, out_weight, precision=highest, preferred_element_type=jnp.float32)
```

```python
import functools

import jax
import jax.numpy as jnp
from jax import lax
from jax.experimental import pallas as pl
from jax.experimental.pallas import tpu as pltpu
from jax.sharding import PartitionSpec as P

MESH = pl.DeviceIdType.MESH
F32 = jnp.float32
BF16 = jnp.bfloat16
HIGHEST = lax.Precision.HIGHEST
DH = 128
NY = 4
TILE = 256


def phi(a):
    return jnp.where(a > 0, a + 1.0, jnp.exp(jnp.minimum(a, 0.0)))


def rc(src, dst, send_sem, recv_sem, dev):
    return pltpu.make_async_remote_copy(
        src_ref=src, dst_ref=dst, send_sem=send_sem, recv_sem=recv_sem,
        device_id=dev, device_id_type=MESH,
    )


def halves(a):
    high = a.astype(BF16)
    return high, (a - high.astype(F32)).astype(BF16)


def kernel(
    nz, nx, q_ref, k_ref, v_ref, w_ref, out_ref,
    w_all, st, sx, ps, r1, yt, yr, s2, r2, fs, full, phiq, numl, denl, att, acat,
    zr_s, zr_r, zl_s, zl_r, yp_s, yp_r, ym_s, ym_r, fd_s, fd_r, sb_s, sb_r,
    e_s, e_r, p1_s, p1_r, yx_s, yx_r, p2_s, p2_r,
    xr_s, xr_r, xl_s, xl_r, gr_s, gr_r, gl_s, gl_r,
):
    s, x = lax.axis_index("seq"), lax.axis_index("tp")
    c = lax.rem(s, 2)
    z = lax.rem(s // 2, nz)
    y = s // (2 * nz)
    tok = q_ref.shape[0]
    rows = 2 * DH // nz

    def at(yy, zz, cc):
        return {"seq": (yy * nz + zz) * 2 + cc}

    def dz(k):
        return lax.rem(z + (k + nz), nz)

    def dy(k):
        return lax.rem(y + (k + NY), NY)

    sib = at(y, z, 1 - c)
    right, left = {"tp": lax.rem(x + 1, nx)}, {"tp": lax.rem(x + nx - 1, nx)}

    barrier = pltpu.get_barrier_semaphore()
    pl.semaphore_signal(barrier, inc=1, device_id=sib, device_id_type=MESH)
    for dev in (right, left):
        pl.semaphore_signal(barrier, inc=1, device_id=dev, device_id_type=MESH)
    for k in range(1, NY):
        pl.semaphore_signal(barrier, inc=1, device_id=at(dy(k), z, c), device_id_type=MESH)
    for k in range(1, nz):
        pl.semaphore_signal(barrier, inc=1, device_id=at(y, dz(k), c), device_id_type=MESH)

    row8 = lax.broadcasted_iota(jnp.int32, (8, DH), 0)
    per = nz // 2
    for b in range(2):
        totals = jnp.zeros((8, DH), F32)
        for hh in range(2):
            h = 2 * b + hh
            cols = slice(h * DH, (h + 1) * DH)
            pk = phi(k_ref[:, cols])
            state = lax.dot_general(
                pk, v_ref[:, cols], (((0,), (0,)), ((), ())),
                precision=HIGHEST, preferred_element_type=F32,
            )
            st[b, hh * per:(hh + 1) * per, 0:rows, :] = state.reshape(per, rows, DH)
            total = jnp.sum(pk, axis=0, keepdims=True)
            totals = jnp.where(row8 == hh, jnp.broadcast_to(total, (8, DH)), totals)
        st[b, :, rows:rows + 8, :] = jnp.broadcast_to(totals[None], (nz, 8, DH))
    w_all[y, z, c] = w_ref[...]
    yr[y] = jnp.zeros((rows + 8, DH), F32)

    pl.semaphore_wait(barrier, 1 + 2 + (NY - 1) + (nz - 1))

    sends = []

    def go(copy):
        copy.start()
        sends.append(copy)

    half = nz // 2

    def zof(m):
        return z if m == 0 else (dz(-m) if m <= half else dz(m - half))

    def slot(yy, m, cc):
        return w_all.at[yy, zof(m), cc]

    def to_sib(k, m):
        ref = slot(dy(-k), m, c)
        go(rc(ref, ref, sb_s.at[k, m], sb_r.at[k, m], sib))

    def have(m):
        src = w_ref if m == 0 else slot(y, m, c)
        dst = slot(y, m, c)
        go(rc(src, dst, yp_s.at[m], yp_r.at[m], at(dy(1), z, c)))
        go(rc(src, dst, ym_s.at[m], ym_r.at[m], at(dy(-1), z, c)))
        go(rc(src, dst, sb_s.at[0, m], sb_r.at[0, m], sib))

    def z_round(r):
        if r == 0:
            dst = slot(y, 0, c)
            go(rc(w_ref, dst, zr_s.at[0], zr_r.at[0], at(y, dz(1), c)))
            go(rc(w_ref, dst, zl_s.at[0], zl_r.at[0], at(y, dz(-1), c)))
            have(0)
            return
        ref = slot(y, r, c)
        rc(ref, ref, zr_s.at[r - 1], zr_r.at[r - 1], at(y, dz(1), c)).wait_recv()
        if r < half:
            go(rc(ref, ref, zr_s.at[r], zr_r.at[r], at(y, dz(1), c)))
        if r < half:
            ref = slot(y, half + r, c)
            rc(ref, ref, zl_s.at[r - 1], zl_r.at[r - 1], at(y, dz(-1), c)).wait_recv()
            if r < half - 1:
                go(rc(ref, ref, zl_s.at[r], zl_r.at[r], at(y, dz(-1), c)))
        have(r)
        if r < half:
            have(half + r)

    def y_stage(r):
        for m in ((r,) if r in (0, half) else (r, half + r)):
            below, above = slot(dy(-1), m, c), slot(dy(1), m, c)
            rc(below, below, yp_s.at[m], yp_r.at[m], at(dy(1), z, c)).wait_recv()
            if m < half:
                go(rc(below, below, fd_s.at[m], fd_r.at[m], at(dy(1), z, c)))
            to_sib(1, m)
            rc(above, above, ym_s.at[m], ym_r.at[m], at(dy(-1), z, c)).wait_recv()
            if m >= half:
                go(rc(above, above, fd_s.at[m], fd_r.at[m], at(dy(-1), z, c)))
            to_sib(3, m)

    def far_stage(m):
        ref = slot(dy(2), m, c)
        rc(ref, ref, fd_s.at[m], fd_r.at[m], at(dy(1), z, c)).wait_recv()
        to_sib(2, m)

    go(rc(st.at[1 - c], sx, e_s.at[0], e_r.at[0], sib))
    z_round(0)
    rc(st.at[1 - c], sx, e_s.at[0], e_r.at[0], sib).wait_recv()
    ps[...] = st[c] + sx[...]

    def send1(k, carry):
        peer = lax.rem(z + k, nz)
        rc(ps.at[peer], r1.at[z], p1_s.at[k], p1_r.at[k], at(y, peer, c)).start()
        return carry

    lax.fori_loop(1, nz, send1, 0)
    r1[z] = ps[z]

    causal = lax.broadcasted_iota(jnp.int32, (tok, tok), 0) >= lax.broadcasted_iota(
        jnp.int32, (tok, tok), 1
    )
    for h in range(4):
        cols = slice(h * DH, (h + 1) * DH)
        pq, pk = phi(q_ref[:, cols]), phi(k_ref[:, cols])
        scores = lax.dot_general(
            pq, pk, (((1,), (1,)), ((), ())), precision=HIGHEST, preferred_element_type=F32
        )
        scores = jnp.where(causal, scores, 0.0)
        phiq[h] = pq
        numl[h] = jnp.dot(
            scores, v_ref[:, cols], precision=HIGHEST, preferred_element_type=F32
        )
        denl[h] = jnp.broadcast_to(jnp.sum(scores, axis=1, keepdims=True), (tok, DH))

    z_round(1)
    z_round(2)

    def wait1(k, carry):
        origin = lax.rem(z + nz - k, nz)
        rc(ps.at[0], r1.at[origin], p1_s.at[k], p1_r.at[k], at(y, origin, c)).wait_recv()
        return carry

    lax.fori_loop(1, nz, wait1, 0)
    acc = jnp.zeros((rows + 8, DH), F32)
    for i in range(nz):
        s2[i] = acc
        acc = acc + r1[i]
    yt[...] = acc
    for k in range(1, NY):
        go(rc(yt, yr.at[y], yx_s.at[k], yx_r.at[k], at(dy(k), z, c)))
    z_round(3)
    y_stage(0)
    for k in range(1, NY):
        rc(yt, yr.at[dy(-k)], yx_s.at[k], yx_r.at[k], at(dy(k), z, c)).wait_recv()
    base = jnp.zeros((rows + 8, DH), F32)
    for yy in range(NY):
        base = base + jnp.where(yy < y, yr[yy], 0.0)
    for i in range(nz):
        s2[i] = s2[i] + base

    def send2(k, carry):
        peer = lax.rem(z + k, nz)
        rc(
            s2.at[peer, pl.ds(0, rows)], r2.at[z, pl.ds(0, rows)],
            p2_s.at[k], p2_r.at[k], at(y, peer, c),
        ).start()
        return carry

    lax.fori_loop(1, nz, send2, 0)
    r2[z, 0:rows, :] = s2[z, 0:rows, :]
    r2[:, rows:rows + 8, :] = jnp.broadcast_to(s2[z, rows:rows + 8, :][None], (nz, 8, DH))

    z_round(4)
    y_stage(1)
    z_round(5)
    y_stage(2)
    z_round(6)
    y_stage(3)

    def wait2(k, carry):
        origin = lax.rem(z + nz - k, nz)
        rc(
            s2.at[0, pl.ds(0, rows)], r2.at[origin, pl.ds(0, rows)],
            p2_s.at[k], p2_r.at[k], at(y, origin, c),
        ).wait_recv()
        return carry

    lax.fori_loop(1, nz, wait2, 0)
    fs[...] = r2[...] + jnp.where(c == 0, st[c], 0.0)
    go(rc(fs, full.at[c], e_s.at[1], e_r.at[1], sib))
    full[c] = r2[...] + jnp.where(c == 1, sx[...], 0.0)

    for t in range(4):
        h, hh = lax.rem(2 * c + t, 4), t % 2
        b = c if t < 2 else 1 - c
        if t == 2:
            rc(fs, full.at[1 - c], e_s.at[1], e_r.at[1], sib).wait_recv()
        prior = full[b, hh * per:(hh + 1) * per, 0:rows, :].reshape(DH, DH)
        total = full[b, 0, rows + hh:rows + hh + 1, :]
        pq = phiq[h]
        num = numl[h] + jnp.dot(pq, prior, precision=HIGHEST, preferred_element_type=F32)
        den = denl[h] + jnp.sum(pq * total, axis=1, keepdims=True)
        att[x, h] = num / den
        go(rc(att.at[x, h], att.at[x, h], xr_s.at[t], xr_r.at[t], right))
        go(rc(att.at[x, h], att.at[x, h], xl_s.at[t], xl_r.at[t], left))

    z_round(7)
    y_stage(4)
    z_round(8)

    xl, xr, xf = lax.rem(x + nx - 1, nx), lax.rem(x + 1, nx), lax.rem(x + 2, nx)
    for t in range(4):
        h = lax.rem(2 * c + t, 4)
        ref = att.at[xl, h]
        rc(ref, ref, xr_s.at[t], xr_r.at[t], right).wait_recv()
        if t % 2 == 0:
            go(rc(ref, ref, gr_s.at[t], gr_r.at[t], right))
        ref = att.at[xr, h]
        rc(ref, ref, xl_s.at[t], xl_r.at[t], left).wait_recv()
        if t % 2 == 1:
            go(rc(ref, ref, gl_s.at[t], gl_r.at[t], left))

    for r in range(5, half + 1):
        y_stage(r)
    for m in range(nz):
        far_stage(m)
    for t in range(4):
        h = lax.rem(2 * c + t, 4)
        ref = att.at[xf, h]
        if t % 2 == 0:
            rc(ref, ref, gr_s.at[t], gr_r.at[t], right).wait_recv()
        else:
            rc(ref, ref, gl_s.at[t], gl_r.at[t], left).wait_recv()
    for k in range(NY):
        for m in range(nz):
            ref = slot(dy(-k), m, 1 - c)
            rc(ref, ref, sb_s.at[k, m], sb_r.at[k, m], sib).wait_recv()

    for xx in range(nx):
        for h in range(4):
            high, low = halves(att[xx, h])
            acat[xx, 0:tok, h * DH:(h + 1) * DH] = high
            acat[xx, tok:2 * tok, h * DH:(h + 1) * DH] = low

    def tile(n, carry):
        cols = pl.ds(pl.multiple_of(n * TILE, TILE), TILE)
        total = jnp.zeros((tok, TILE), F32)
        for xx in range(nx):
            wt = w_all[xx, :, :, :, cols].reshape(4 * DH, TILE)
            high, low = halves(wt)
            both = jnp.dot(acat[xx], high, preferred_element_type=F32)
            total = total + (
                both[0:tok] + both[tok:2 * tok]
                + jnp.dot(acat[xx, 0:tok, :], low, preferred_element_type=F32)
            )
        out_ref[:, cols] = total
        return carry

    lax.fori_loop(0, out_ref.shape[1] // TILE, tile, 0)

    for copy in sends:
        copy.wait_send()

    def sent(k, carry):
        peer = lax.rem(z + k, nz)
        rc(ps.at[peer], r1.at[z], p1_s.at[k], p1_r.at[k], at(y, peer, c)).wait_send()
        rc(
            s2.at[peer, pl.ds(0, rows)], r2.at[z, pl.ds(0, rows)],
            p2_s.at[k], p2_r.at[k], at(y, peer, c),
        ).wait_send()
        return carry

    lax.fori_loop(1, nz, sent, 0)


def solution(mesh):
    nz, nx = mesh.shape["seq"] // (2 * NY), mesh.shape["tp"]

    def shards(queries, keys, values, out_weight):
        tok = queries.shape[0]
        depth, columns = out_weight.shape
        part = (nz, 2 * DH // nz + 8, DH)
        dma = pltpu.SemaphoreType.DMA
        vmem = pl.BlockSpec(memory_space=pltpu.VMEM)
        return pl.pallas_call(
            functools.partial(kernel, nz, nx),
            out_shape=jax.ShapeDtypeStruct((tok, columns), F32),
            in_specs=[vmem] * 4,
            out_specs=vmem,
            scratch_shapes=[
                pltpu.VMEM((NY, nz, 2, depth, columns), F32),
                pltpu.VMEM((2,) + part, F32),
                pltpu.VMEM(part, F32),
                pltpu.VMEM(part, F32),
                pltpu.VMEM(part, F32),
                pltpu.VMEM(part[1:], F32),
                pltpu.VMEM((NY,) + part[1:], F32),
                pltpu.VMEM(part, F32),
                pltpu.VMEM(part, F32),
                pltpu.VMEM(part, F32),
                pltpu.VMEM((2,) + part, F32),
                pltpu.VMEM((4, tok, DH), F32),
                pltpu.VMEM((4, tok, DH), F32),
                pltpu.VMEM((4, tok, DH), F32),
                pltpu.VMEM((nx, 4, tok, DH), F32),
                pltpu.VMEM((nx, 2 * tok, 4 * DH), BF16),
            ]
            + [dma((nz // 2,))] * 4
            + [dma((nz,))] * 6
            + [dma((NY, nz))] * 2
            + [dma((2,))] * 2
            + [dma((nz,))] * 2
            + [dma((NY,))] * 2
            + [dma((nz,))] * 2
            + [dma((4,))] * 8,
            compiler_params=pltpu.CompilerParams(
                collective_id=0, has_side_effects=True, vmem_limit_bytes=48 << 20
            ),
        )(queries, keys, values, out_weight)

    return jax.shard_map(
        shards,
        mesh=mesh,
        in_specs=(P("seq", "tp"),) * 4,
        out_specs=P("seq", "tp"),
        check_vma=False,
    )
```

```python
import functools

import jax
import jax.numpy as jnp
from jax import lax
from jax.experimental import pallas as pl
from jax.experimental.pallas import tpu as pltpu
from jax.sharding import PartitionSpec as P

MESH = pl.DeviceIdType.MESH
F32 = jnp.float32
BF16 = jnp.bfloat16
DH = 128
NY = 4
TILE = 256


def phi(a):
    return jnp.where(a > 0, a + 1.0, jnp.exp(jnp.minimum(a, 0.0)))


def rc(src, dst, send_sem, recv_sem, dev):
    return pltpu.make_async_remote_copy(
        src_ref=src, dst_ref=dst, send_sem=send_sem, recv_sem=recv_sem,
        device_id=dev, device_id_type=MESH,
    )


def halves(a):
    high = a.astype(BF16)
    return high, (a - high.astype(F32)).astype(BF16)


def dot3(a, b, dims):
    (ah, al), (bh, bl) = a, b

    def one(p, r):
        return lax.dot_general(p, r, (dims, ((), ())), preferred_element_type=F32)

    return one(ah, bh) + (one(al, bh) + one(ah, bl))


def kernel(
    nz, nx, q_hbm, k_hbm, v_hbm, w_hbm, out_ref,
    w_all, q_ref, k_ref, v_ref, st, tst, sx, tsx, ps, pt, r1, rt1, yt, yr, s2, r2, fs, full,
    ft, ftot, phiq, qh, ql, numl, denl, att, acat,
    in_s, tok_r, tok_l,
    zr_s, zr_r, zl_s, zl_r, yp_s, yp_r, ym_s, ym_r, fd_s, fd_r, sb_s, sb_r,
    e_s, e_r, p1_s, p1_r, pt_s, pt_r, yx_s, yx_r, p2_s, p2_r,
    xr_s, xr_r, xl_s, xl_r, gr_s, gr_r, gl_s, gl_r,
):
    s, x = lax.axis_index("seq"), lax.axis_index("tp")
    c = lax.rem(s, 2)
    z = lax.rem(s // 2, nz)
    y = s // (2 * nz)
    tok = q_ref.shape[0]
    rows = 2 * DH // nz

    def at(yy, zz, cc):
        return {"seq": (yy * nz + zz) * 2 + cc}

    def dz(k):
        return lax.rem(z + (k + nz), nz)

    def dy(k):
        return lax.rem(y + (k + NY), NY)

    sib = at(y, z, 1 - c)
    right, left = {"tp": lax.rem(x + 1, nx)}, {"tp": lax.rem(x + nx - 1, nx)}
    up, down = at(y, dz(1), c), at(y, dz(-1), c)
    half = nz // 2

    barrier = pltpu.get_barrier_semaphore()
    near = [sib, right, left, up, down] + [at(dy(k), z, c) for k in range(1, NY)]
    for dev in near:
        pl.semaphore_signal(barrier, inc=1, device_id=dev, device_id_type=MESH)
    inputs = [
        pltpu.make_async_copy(src, dst, in_s.at[i])
        for i, (src, dst) in enumerate(
            ((w_hbm, w_all.at[y, z, c]), (k_hbm, k_ref), (v_hbm, v_ref), (q_hbm, q_ref))
        )
    ]
    for copy in inputs:
        copy.start()
    pl.semaphore_wait(barrier, len(near))

    def token(r):
        if r > 1:
            pl.semaphore_wait(tok_l.at[r], 1)
        if r < half:
            pl.semaphore_signal(tok_l.at[r + 1], inc=1, device_id=down, device_id_type=MESH)
        if r < half:
            if r > 1:
                pl.semaphore_wait(tok_r.at[r], 1)
            if r < half - 1:
                pl.semaphore_signal(tok_r.at[r + 1], inc=1, device_id=up, device_id_type=MESH)

    sends = []

    def go(copy):
        copy.start()
        sends.append(copy)

    def zof(m):
        return z if m == 0 else (dz(-m) if m <= half else dz(m - half))

    def slot(yy, m, cc):
        return w_all.at[yy, zof(m), cc]

    def to_sib(k, m):
        ref = slot(dy(-k), m, c)
        go(rc(ref, ref, sb_s.at[k, m], sb_r.at[k, m], sib))

    def have(m):
        src = dst = slot(y, m, c)
        go(rc(src, dst, yp_s.at[m], yp_r.at[m], at(dy(1), z, c)))
        go(rc(src, dst, ym_s.at[m], ym_r.at[m], at(dy(-1), z, c)))
        go(rc(src, dst, sb_s.at[0, m], sb_r.at[0, m], sib))

    def z_round(r):
        if r == 0:
            dst = slot(y, 0, c)
            go(rc(dst, dst, zr_s.at[0], zr_r.at[0], at(y, dz(1), c)))
            go(rc(dst, dst, zl_s.at[0], zl_r.at[0], at(y, dz(-1), c)))
            have(0)
            return
        ref = slot(y, r, c)
        rc(ref, ref, zr_s.at[r - 1], zr_r.at[r - 1], at(y, dz(1), c)).wait_recv()
        if r < half:
            go(rc(ref, ref, zr_s.at[r], zr_r.at[r], at(y, dz(1), c)))
        if r < half:
            ref = slot(y, half + r, c)
            rc(ref, ref, zl_s.at[r - 1], zl_r.at[r - 1], at(y, dz(-1), c)).wait_recv()
            if r < half - 1:
                go(rc(ref, ref, zl_s.at[r], zl_r.at[r], at(y, dz(-1), c)))
        have(r)
        if r < half:
            have(half + r)

    def y_stage(r):
        for m in ((r,) if r in (0, half) else (r, half + r)):
            below, above = slot(dy(-1), m, c), slot(dy(1), m, c)
            rc(below, below, yp_s.at[m], yp_r.at[m], at(dy(1), z, c)).wait_recv()
            if m < half:
                go(rc(below, below, fd_s.at[m], fd_r.at[m], at(dy(1), z, c)))
            to_sib(1, m)
            rc(above, above, ym_s.at[m], ym_r.at[m], at(dy(-1), z, c)).wait_recv()
            if m >= half:
                go(rc(above, above, fd_s.at[m], fd_r.at[m], at(dy(-1), z, c)))
            to_sib(3, m)

    def far_stage(m):
        ref = slot(dy(2), m, c)
        rc(ref, ref, fd_s.at[m], fd_r.at[m], at(dy(1), z, c)).wait_recv()
        to_sib(2, m)

    token(1)
    inputs[0].wait()
    z_round(0)
    inputs[1].wait()
    inputs[2].wait()
    row8 = lax.broadcasted_iota(jnp.int32, (8, DH), 0)
    per = nz // 2
    hops = ((2, 3), (4, 5), (6,), (7, 8))
    for t in range(4):
        b, hh = (1 - c if t < 2 else c), t % 2
        cols = pl.ds(pl.multiple_of((2 * b + hh) * DH, DH), DH)
        pk = phi(k_ref[:, cols])
        state = dot3(halves(pk), halves(v_ref[:, cols]), ((0,), (0,)))
        st[b, hh * per:(hh + 1) * per] = state.reshape(per, rows, DH)
        total = jnp.broadcast_to(jnp.sum(pk, axis=0, keepdims=True), (8, DH))
        if hh == 0:
            totals = total
        else:
            tst[b] = jnp.where(row8 == 0, totals, total)
        if t == 1:
            go(rc(st.at[b], sx, e_s.at[0], e_r.at[0], sib))
            go(rc(tst.at[b], tsx, e_s.at[1], e_r.at[1], sib))
        for r in hops[t]:
            token(r)
        if t == 2:
            z_round(1)
    rc(st.at[1 - c], sx, e_s.at[0], e_r.at[0], sib).wait_recv()
    rc(tst.at[1 - c], tsx, e_s.at[1], e_r.at[1], sib).wait_recv()
    ps[...] = st[c] + sx[...]
    pt[...] = tst[c, 0:2] + tsx[0:2]

    def send1(k, carry):
        peer = lax.rem(z + k, nz)
        rc(ps.at[peer], r1.at[z], p1_s.at[k], p1_r.at[k], at(y, peer, c)).start()
        rc(pt, rt1.at[z], pt_s.at[k], pt_r.at[k], at(y, peer, c)).start()
        return carry

    lax.fori_loop(1, nz, send1, 0)
    r1[z] = ps[z]
    rt1[z] = pt[...]
    yr[y] = jnp.zeros((rows + 8, DH), F32)
    z_round(2)

    inputs[3].wait()
    causal = lax.broadcasted_iota(jnp.int32, (tok, tok), 0) >= lax.broadcasted_iota(
        jnp.int32, (tok, tok), 1
    )
    for h in range(4):
        cols = slice(h * DH, (h + 1) * DH)
        pq = phi(q_ref[:, cols])
        parts = halves(pq)
        scores = dot3(parts, halves(phi(k_ref[:, cols])), ((1,), (1,)))
        scores = jnp.where(causal, scores, 0.0)
        phiq[h] = pq
        qh[h], ql[h] = parts
        numl[h] = dot3(halves(scores), halves(v_ref[:, cols]), ((1,), (0,)))
        denl[h] = jnp.broadcast_to(jnp.sum(scores, axis=1, keepdims=True), (tok, DH))

    z_round(3)

    def wait1(k, carry):
        origin = lax.rem(z + nz - k, nz)
        rc(ps.at[0], r1.at[origin], p1_s.at[k], p1_r.at[k], at(y, origin, c)).wait_recv()
        rc(pt, rt1.at[origin], pt_s.at[k], pt_r.at[k], at(y, origin, c)).wait_recv()
        return carry

    lax.fori_loop(1, nz, wait1, 0)
    acc = jnp.zeros((rows, DH), F32)
    acct = jnp.zeros((2, DH), F32)
    mine = jnp.zeros((2, DH), F32)
    for i in range(nz):
        s2[i] = acc
        acc = acc + r1[i]
        mine = mine + jnp.where(i < z, rt1[i], 0.0)
        acct = acct + rt1[i]
    yt[0:rows, :] = acc
    yt[rows:rows + 2, :] = acct
    yt[rows + 2:rows + 8, :] = jnp.zeros((6, DH), F32)
    for k in range(1, NY):
        go(rc(yt, yr.at[y], yx_s.at[k], yx_r.at[k], at(dy(k), z, c)))
    z_round(4)
    for k in range(1, NY):
        rc(yt, yr.at[dy(-k)], yx_s.at[k], yx_r.at[k], at(dy(k), z, c)).wait_recv()
    base = jnp.zeros((rows + 8, DH), F32)
    for yy in range(NY):
        base = base + jnp.where(yy < y, yr[yy], 0.0)
    for i in range(nz):
        s2[i] = s2[i] + base[0:rows]

    def send2(k, carry):
        peer = lax.rem(z + k, nz)
        rc(s2.at[peer], r2.at[z], p2_s.at[k], p2_r.at[k], at(y, peer, c)).start()
        return carry

    lax.fori_loop(1, nz, send2, 0)
    r2[z] = s2[z]

    mine = mine + base[rows:rows + 2]
    ft[...] = jnp.zeros_like(ft)
    ft[0:2, :] = mine + jnp.where(c == 0, tst[c, 0:2], 0.0)
    go(rc(ft, ftot.at[c], e_s.at[2], e_r.at[2], sib))
    ftot[c, 0:2, :] = mine + jnp.where(c == 1, tsx[0:2], 0.0)
    z_round(5)
    rc(ft, ftot.at[1 - c], e_s.at[2], e_r.at[2], sib).wait_recv()
    for h in range(4):
        total = ftot[h // 2, h % 2:h % 2 + 1, :]
        denl[h] = denl[h] + jnp.sum(phiq[h] * total, axis=1, keepdims=True)

    z_round(6)
    y_stage(0)
    z_round(7)
    y_stage(1)
    y_stage(2)
    z_round(8)
    y_stage(3)

    def wait2(k, carry):
        origin = lax.rem(z + nz - k, nz)
        rc(s2.at[0], r2.at[origin], p2_s.at[k], p2_r.at[k], at(y, origin, c)).wait_recv()
        return carry

    lax.fori_loop(1, nz, wait2, 0)
    fs[...] = r2[...] + jnp.where(c == 0, st[c], 0.0)
    go(rc(fs, full.at[c], e_s.at[3], e_r.at[3], sib))
    full[c] = r2[...] + jnp.where(c == 1, sx[...], 0.0)

    for t in range(4):
        h, hh = lax.rem(2 * c + t, 4), t % 2
        b = c if t < 2 else 1 - c
        if t == 2:
            rc(fs, full.at[1 - c], e_s.at[3], e_r.at[3], sib).wait_recv()
        prior = halves(full[b, hh * per:(hh + 1) * per].reshape(DH, DH))
        num = numl[h] + dot3((qh[h], ql[h]), prior, ((1,), (0,)))
        att[x, h] = num / denl[h]
        go(rc(att.at[x, h], att.at[x, h], xr_s.at[t], xr_r.at[t], right))
        go(rc(att.at[x, h], att.at[x, h], xl_s.at[t], xl_r.at[t], left))

    y_stage(4)
    y_stage(5)
    y_stage(6)
    xl, xr, xf = lax.rem(x + nx - 1, nx), lax.rem(x + 1, nx), lax.rem(x + 2, nx)
    for t in range(4):
        h = lax.rem(2 * c + t, 4)
        ref = att.at[xl, h]
        rc(ref, ref, xr_s.at[t], xr_r.at[t], right).wait_recv()
        if t % 2 == 0:
            go(rc(ref, ref, gr_s.at[t], gr_r.at[t], right))
        ref = att.at[xr, h]
        rc(ref, ref, xl_s.at[t], xl_r.at[t], left).wait_recv()
        if t % 2 == 1:
            go(rc(ref, ref, gl_s.at[t], gl_r.at[t], left))

    for r in range(7, half + 1):
        y_stage(r)
    for m in range(nz):
        far_stage(m)
    for t in range(4):
        h = lax.rem(2 * c + t, 4)
        ref = att.at[xf, h]
        if t % 2 == 0:
            rc(ref, ref, gr_s.at[t], gr_r.at[t], right).wait_recv()
        else:
            rc(ref, ref, gl_s.at[t], gl_r.at[t], left).wait_recv()
    for k in range(NY):
        for m in range(nz):
            ref = slot(dy(-k), m, 1 - c)
            rc(ref, ref, sb_s.at[k, m], sb_r.at[k, m], sib).wait_recv()

    for xx in range(nx):
        for h in range(4):
            high, low = halves(att[xx, h])
            acat[xx, 0:tok, h * DH:(h + 1) * DH] = high
            acat[xx, tok:2 * tok, h * DH:(h + 1) * DH] = low

    def tile(n, carry):
        cols = pl.ds(pl.multiple_of(n * TILE, TILE), TILE)
        total = jnp.zeros((tok, TILE), F32)
        for xx in range(nx):
            wt = w_all[xx, :, :, :, cols].reshape(4 * DH, TILE)
            high, low = halves(wt)
            both = jnp.dot(acat[xx], high, preferred_element_type=F32)
            total = total + (
                both[0:tok] + both[tok:2 * tok]
                + jnp.dot(acat[xx, 0:tok, :], low, preferred_element_type=F32)
            )
        out_ref[:, cols] = total
        return carry

    lax.fori_loop(0, out_ref.shape[1] // TILE, tile, 0)

    for copy in sends:
        copy.wait_send()

    def sent(k, carry):
        peer = lax.rem(z + k, nz)
        dev = at(y, peer, c)
        rc(ps.at[peer], r1.at[z], p1_s.at[k], p1_r.at[k], dev).wait_send()
        rc(pt, rt1.at[z], pt_s.at[k], pt_r.at[k], dev).wait_send()
        rc(s2.at[peer], r2.at[z], p2_s.at[k], p2_r.at[k], dev).wait_send()
        return carry

    lax.fori_loop(1, nz, sent, 0)


def solution(mesh):
    nz, nx = mesh.shape["seq"] // (2 * NY), mesh.shape["tp"]

    def shards(queries, keys, values, out_weight):
        tok = queries.shape[0]
        depth, columns = out_weight.shape
        part = (nz, 2 * DH // nz, DH)
        dma = pltpu.SemaphoreType.DMA
        vmem = pl.BlockSpec(memory_space=pltpu.VMEM)
        return pl.pallas_call(
            functools.partial(kernel, nz, nx),
            out_shape=jax.ShapeDtypeStruct((tok, columns), F32),
            in_specs=[pl.BlockSpec(memory_space=pltpu.HBM)] * 4,
            out_specs=vmem,
            scratch_shapes=[
                pltpu.VMEM((NY, nz, 2, depth, columns), F32),
                pltpu.VMEM((tok, 4 * DH), F32),
                pltpu.VMEM((tok, 4 * DH), F32),
                pltpu.VMEM((tok, 4 * DH), F32),
                pltpu.VMEM((2,) + part, F32),
                pltpu.VMEM((2, 8, DH), F32),
                pltpu.VMEM(part, F32),
                pltpu.VMEM((8, DH), F32),
                pltpu.VMEM(part, F32),
                pltpu.VMEM((2, DH), F32),
                pltpu.VMEM(part, F32),
                pltpu.VMEM((nz, 2, DH), F32),
                pltpu.VMEM((part[1] + 8, DH), F32),
                pltpu.VMEM((NY, part[1] + 8, DH), F32),
                pltpu.VMEM(part, F32),
                pltpu.VMEM(part, F32),
                pltpu.VMEM(part, F32),
                pltpu.VMEM((2,) + part, F32),
                pltpu.VMEM((8, DH), F32),
                pltpu.VMEM((2, 8, DH), F32),
                pltpu.VMEM((4, tok, DH), F32),
                pltpu.VMEM((4, tok, DH), BF16),
                pltpu.VMEM((4, tok, DH), BF16),
                pltpu.VMEM((4, tok, DH), F32),
                pltpu.VMEM((4, tok, DH), F32),
                pltpu.VMEM((nx, 4, tok, DH), F32),
                pltpu.VMEM((nx, 2 * tok, 4 * DH), BF16),
                dma((4,)),
                pltpu.SemaphoreType.REGULAR((nz // 2 + 1,)),
                pltpu.SemaphoreType.REGULAR((nz // 2 + 1,)),
            ]
            + [dma((nz // 2,))] * 4
            + [dma((nz,))] * 6
            + [dma((NY, nz))] * 2
            + [dma((4,))] * 2
            + [dma((nz,))] * 4
            + [dma((NY,))] * 2
            + [dma((nz,))] * 2
            + [dma((4,))] * 8,
            compiler_params=pltpu.CompilerParams(
                collective_id=0, has_side_effects=True, vmem_limit_bytes=67043328
            ),
        )(queries, keys, values, out_weight)

    return jax.shard_map(
        shards,
        mesh=mesh,
        in_specs=(P("seq", "tp"),) * 4,
        out_specs=P("seq", "tp"),
        check_vma=False,
    )
```

```python
import functools

import jax
import jax.numpy as jnp
from jax import lax
from jax.experimental import pallas as pl
from jax.experimental.pallas import tpu as pltpu
from jax.sharding import PartitionSpec as P

MESH = pl.DeviceIdType.MESH
F32 = jnp.float32
BF16 = jnp.bfloat16
DH = 128
NY = 4
TILE = 256


def phi(a):
    return jnp.where(a > 0, a + 1.0, jnp.exp(jnp.minimum(a, 0.0)))


def rc(src, dst, send_sem, recv_sem, dev):
    return pltpu.make_async_remote_copy(
        src_ref=src, dst_ref=dst, send_sem=send_sem, recv_sem=recv_sem,
        device_id=dev, device_id_type=MESH,
    )


def halves(a):
    high = a.astype(BF16)
    return high, (a - high.astype(F32)).astype(BF16)


def dot3(a, b, dims):
    (ah, al), (bh, bl) = a, b

    def one(p, r):
        return lax.dot_general(p, r, (dims, ((), ())), preferred_element_type=F32)

    return one(ah, bh) + (one(al, bh) + one(ah, bl))


def kernel(
    nz, nx, q_hbm, k_hbm, v_hbm, w_hbm, out_ref,
    w_all, q_ref, k_ref, v_ref, st, tst, sx, tsx, ps, pt, r1, rt1, yt, yr, s2, r2, fs, full,
    ft, ftot, phiq, qh, ql, numl, denl, att, acat,
    in_s, tok_r, tok_l,
    zr_s, zr_r, zl_s, zl_r, yp_s, yp_r, ym_s, ym_r, fd_s, fd_r, sb_s, sb_r,
    e_s, e_r, p1_s, p1_r, pt_s, pt_r, yx_s, yx_r, p2_s, p2_r,
    xr_s, xr_r, xl_s, xl_r, gr_s, gr_r, gl_s, gl_r,
):
    s, x = lax.axis_index("seq"), lax.axis_index("tp")
    c = lax.rem(s, 2)
    z = lax.rem(s // 2, nz)
    y = s // (2 * nz)
    tok = q_ref.shape[0]
    rows = 2 * DH // nz

    def at(yy, zz, cc):
        return {"seq": (yy * nz + zz) * 2 + cc}

    def dz(k):
        return lax.rem(z + (k + nz), nz)

    def dy(k):
        return lax.rem(y + (k + NY), NY)

    sib = at(y, z, 1 - c)
    right, left = {"tp": lax.rem(x + 1, nx)}, {"tp": lax.rem(x + nx - 1, nx)}
    up, down = at(y, dz(1), c), at(y, dz(-1), c)
    up2, down2 = at(y, dz(2), c), at(y, dz(-2), c)
    half = nz // 2

    barrier = pltpu.get_barrier_semaphore()
    near = [sib, right, left, up, down, up2, down2] + [at(dy(k), z, c) for k in range(1, NY)]
    for dev in near:
        pl.semaphore_signal(barrier, inc=1, device_id=dev, device_id_type=MESH)
    inputs = [
        pltpu.make_async_copy(src, dst, in_s.at[i])
        for i, (src, dst) in enumerate(
            ((w_hbm, w_all.at[y, z, c]), (k_hbm, k_ref), (v_hbm, v_ref), (q_hbm, q_ref))
        )
    ]
    for copy in inputs:
        copy.start()
    pl.semaphore_wait(barrier, len(near))

    def token(j):
        if j > 1:
            pl.semaphore_wait(tok_l.at[j - 1], 1)
            pl.semaphore_wait(tok_r.at[j - 1], 1)
        if 2 * j < half:
            pl.semaphore_signal(tok_l.at[j], inc=1, device_id=down2, device_id_type=MESH)
            pl.semaphore_signal(tok_r.at[j], inc=1, device_id=up2, device_id_type=MESH)

    sends = []

    def go(copy):
        copy.start()
        sends.append(copy)

    def zof(m):
        return z if m == 0 else (dz(-m) if m <= half else dz(m - half))

    def slot(yy, m, cc):
        return w_all.at[yy, zof(m), cc]

    def to_sib(k, m):
        ref = slot(dy(-k), m, c)
        go(rc(ref, ref, sb_s.at[k, m], sb_r.at[k, m], sib))

    def have(m):
        src = dst = slot(y, m, c)
        go(rc(src, dst, yp_s.at[m], yp_r.at[m], at(dy(1), z, c)))
        go(rc(src, dst, ym_s.at[m], ym_r.at[m], at(dy(-1), z, c)))
        go(rc(src, dst, sb_s.at[0, m], sb_r.at[0, m], sib))

    def pass_on(m, d):
        ref = slot(y, m, c)
        if m <= half:
            if d + 2 <= half:
                go(rc(ref, ref, zr_s.at[d + 1], zr_r.at[d + 1], up2))
            if d + 1 <= half:
                go(rc(ref, ref, zr_s.at[d], zr_r.at[d], up))
        else:
            if d + 2 < half:
                go(rc(ref, ref, zl_s.at[d + 1], zl_r.at[d + 1], down2))
            if d + 1 < half:
                go(rc(ref, ref, zl_s.at[d], zl_r.at[d], down))

    def z_round(r):
        if r == 0:
            ref = slot(y, 0, c)
            go(rc(ref, ref, zr_s.at[1], zr_r.at[1], up2))
            go(rc(ref, ref, zl_s.at[1], zl_r.at[1], down2))
            go(rc(ref, ref, zr_s.at[0], zr_r.at[0], up))
            go(rc(ref, ref, zl_s.at[0], zl_r.at[0], down))
            have(0)
            return
        for d in (2 * r, 2 * r - 1):
            ref = slot(y, d, c)
            rc(ref, ref, zr_s.at[d - 1], zr_r.at[d - 1], up).wait_recv()
            if d == 2 * r:
                pass_on(d, d)
            if d < half:
                ref = slot(y, half + d, c)
                rc(ref, ref, zl_s.at[d - 1], zl_r.at[d - 1], down).wait_recv()
                if d == 2 * r:
                    pass_on(half + d, d)
        if r not in (3,):
            spread(r)

    def spread(r):
        for d in (2 * r - 1, 2 * r):
            have(d)
            if d < half:
                have(half + d)

    late = []

    def push(k, m):
        late.append((k, m))

    def flush():
        for k, m in late:
            to_sib(k, m)
        late.clear()

    def y_stage(r):
        for m in ((r,) if r in (0, half) else (r, half + r)):
            below, above = slot(dy(-1), m, c), slot(dy(1), m, c)
            rc(below, below, yp_s.at[m], yp_r.at[m], at(dy(1), z, c)).wait_recv()
            if m < half:
                go(rc(below, below, fd_s.at[m], fd_r.at[m], at(dy(1), z, c)))
            push(1, m)
            rc(above, above, ym_s.at[m], ym_r.at[m], at(dy(-1), z, c)).wait_recv()
            if m >= half:
                go(rc(above, above, fd_s.at[m], fd_r.at[m], at(dy(-1), z, c)))
            push(3, m)

    def far_stage(m):
        ref = slot(dy(2), m, c)
        rc(ref, ref, fd_s.at[m], fd_r.at[m], at(dy(1), z, c)).wait_recv()
        to_sib(2, m)

    token(1)
    inputs[0].wait()
    z_round(0)
    inputs[1].wait()
    inputs[2].wait()
    row8 = lax.broadcasted_iota(jnp.int32, (8, DH), 0)
    per = nz // 2
    hops = ((2,), (3,), (4,), ())
    for t in range(4):
        b, hh = (1 - c if t < 2 else c), t % 2
        cols = pl.ds(pl.multiple_of((2 * b + hh) * DH, DH), DH)
        pk = phi(k_ref[:, cols])
        state = dot3(halves(pk), halves(v_ref[:, cols]), ((0,), (0,)))
        st[b, hh * per:(hh + 1) * per] = state.reshape(per, rows, DH)
        total = jnp.broadcast_to(jnp.sum(pk, axis=0, keepdims=True), (8, DH))
        if hh == 0:
            totals = total
        else:
            tst[b] = jnp.where(row8 == 0, totals, total)
        if t == 1:
            go(rc(st.at[b], sx, e_s.at[0], e_r.at[0], sib))
            go(rc(tst.at[b], tsx, e_s.at[1], e_r.at[1], sib))
        for r in hops[t]:
            token(r)
        if t == 1:
            z_round(1)
    rc(st.at[1 - c], sx, e_s.at[0], e_r.at[0], sib).wait_recv()
    rc(tst.at[1 - c], tsx, e_s.at[1], e_r.at[1], sib).wait_recv()
    ps[...] = st[c] + sx[...]
    pt[...] = tst[c, 0:2] + tsx[0:2]

    def send1(k, carry):
        peer = lax.rem(z + k, nz)
        rc(ps.at[peer], r1.at[z], p1_s.at[k], p1_r.at[k], at(y, peer, c)).start()
        rc(pt, rt1.at[z], pt_s.at[k], pt_r.at[k], at(y, peer, c)).start()
        return carry

    lax.fori_loop(1, nz, send1, 0)
    r1[z] = ps[z]
    rt1[z] = pt[...]
    yr[y] = jnp.zeros((rows + 8, DH), F32)

    inputs[3].wait()
    causal = lax.broadcasted_iota(jnp.int32, (tok, tok), 0) >= lax.broadcasted_iota(
        jnp.int32, (tok, tok), 1
    )
    for h in range(4):
        cols = slice(h * DH, (h + 1) * DH)
        pq = phi(q_ref[:, cols])
        parts = halves(pq)
        scores = dot3(parts, halves(phi(k_ref[:, cols])), ((1,), (1,)))
        scores = jnp.where(causal, scores, 0.0)
        phiq[h] = pq
        qh[h], ql[h] = parts
        numl[h] = dot3(halves(scores), halves(v_ref[:, cols]), ((1,), (0,)))
        denl[h] = jnp.broadcast_to(jnp.sum(scores, axis=1, keepdims=True), (tok, DH))
        if h == 1:
            z_round(2)

    def wait1(k, carry):
        origin = lax.rem(z + nz - k, nz)
        rc(ps.at[0], r1.at[origin], p1_s.at[k], p1_r.at[k], at(y, origin, c)).wait_recv()
        rc(pt, rt1.at[origin], pt_s.at[k], pt_r.at[k], at(y, origin, c)).wait_recv()
        return carry

    lax.fori_loop(1, nz, wait1, 0)
    acc = jnp.zeros((rows, DH), F32)
    acct = jnp.zeros((2, DH), F32)
    mine = jnp.zeros((2, DH), F32)
    for i in range(nz):
        s2[i] = acc
        acc = acc + r1[i]
        mine = mine + jnp.where(i < z, rt1[i], 0.0)
        acct = acct + rt1[i]
    yt[0:rows, :] = acc
    yt[rows:rows + 2, :] = acct
    yt[rows + 2:rows + 8, :] = jnp.zeros((6, DH), F32)
    for k in range(1, NY):
        go(rc(yt, yr.at[y], yx_s.at[k], yx_r.at[k], at(dy(k), z, c)))
    z_round(3)
    spread(3)
    y_stage(0)
    for k in range(1, NY):
        rc(yt, yr.at[dy(-k)], yx_s.at[k], yx_r.at[k], at(dy(k), z, c)).wait_recv()
    base = jnp.zeros((rows + 8, DH), F32)
    for yy in range(NY):
        base = base + jnp.where(yy < y, yr[yy], 0.0)
    for i in range(nz):
        s2[i] = s2[i] + base[0:rows]

    def send2(k, carry):
        peer = lax.rem(z + k, nz)
        rc(s2.at[peer], r2.at[z], p2_s.at[k], p2_r.at[k], at(y, peer, c)).start()
        return carry

    lax.fori_loop(1, nz, send2, 0)
    r2[z] = s2[z]

    mine = mine + base[rows:rows + 2]
    ft[...] = jnp.zeros_like(ft)
    ft[0:2, :] = mine + jnp.where(c == 0, tst[c, 0:2], 0.0)
    go(rc(ft, ftot.at[c], e_s.at[2], e_r.at[2], sib))
    ftot[c, 0:2, :] = mine + jnp.where(c == 1, tsx[0:2], 0.0)
    z_round(4)
    rc(ft, ftot.at[1 - c], e_s.at[2], e_r.at[2], sib).wait_recv()
    for h in range(4):
        total = ftot[h // 2, h % 2:h % 2 + 1, :]
        denl[h] = denl[h] + jnp.sum(phiq[h] * total, axis=1, keepdims=True)

    for r in range(1, 5):
        y_stage(r)

    def wait2(k, carry):
        origin = lax.rem(z + nz - k, nz)
        rc(s2.at[0], r2.at[origin], p2_s.at[k], p2_r.at[k], at(y, origin, c)).wait_recv()
        return carry

    lax.fori_loop(1, nz, wait2, 0)
    fs[...] = r2[...] + jnp.where(c == 0, st[c], 0.0)
    go(rc(fs, full.at[c], e_s.at[3], e_r.at[3], sib))
    full[c] = r2[...] + jnp.where(c == 1, sx[...], 0.0)

    for t in range(4):
        h, hh = lax.rem(2 * c + t, 4), t % 2
        b = c if t < 2 else 1 - c
        if t == 2:
            rc(fs, full.at[1 - c], e_s.at[3], e_r.at[3], sib).wait_recv()
        prior = halves(full[b, hh * per:(hh + 1) * per].reshape(DH, DH))
        num = numl[h] + dot3((qh[h], ql[h]), prior, ((1,), (0,)))
        att[x, h] = num / denl[h]
        go(rc(att.at[x, h], att.at[x, h], xr_s.at[t], xr_r.at[t], right))
        go(rc(att.at[x, h], att.at[x, h], xl_s.at[t], xl_r.at[t], left))

    flush()
    y_stage(5)
    y_stage(6)
    flush()
    xl, xr, xf = lax.rem(x + nx - 1, nx), lax.rem(x + 1, nx), lax.rem(x + 2, nx)
    for t in range(4):
        h = lax.rem(2 * c + t, 4)
        ref = att.at[xl, h]
        rc(ref, ref, xr_s.at[t], xr_r.at[t], right).wait_recv()
        if t % 2 == 0:
            go(rc(ref, ref, gr_s.at[t], gr_r.at[t], right))
        ref = att.at[xr, h]
        rc(ref, ref, xl_s.at[t], xl_r.at[t], left).wait_recv()
        if t % 2 == 1:
            go(rc(ref, ref, gl_s.at[t], gl_r.at[t], left))
        if t % 2 == 1:
            y_stage(7 + t // 2)
            flush()

    for m in range(nz):
        far_stage(m)
    for t in range(4):
        h = lax.rem(2 * c + t, 4)
        ref = att.at[xf, h]
        if t % 2 == 0:
            rc(ref, ref, gr_s.at[t], gr_r.at[t], right).wait_recv()
        else:
            rc(ref, ref, gl_s.at[t], gl_r.at[t], left).wait_recv()
    for k in range(NY):
        for m in range(nz):
            ref = slot(dy(-k), m, 1 - c)
            rc(ref, ref, sb_s.at[k, m], sb_r.at[k, m], sib).wait_recv()

    for xx in range(nx):
        for h in range(4):
            high, low = halves(att[xx, h])
            acat[xx, 0:tok, h * DH:(h + 1) * DH] = high
            acat[xx, tok:2 * tok, h * DH:(h + 1) * DH] = low

    def tile(n, carry):
        cols = pl.ds(pl.multiple_of(n * TILE, TILE), TILE)
        total = jnp.zeros((tok, TILE), F32)
        for xx in range(nx):
            wt = w_all[xx, :, :, :, cols].reshape(4 * DH, TILE)
            high, low = halves(wt)
            both = jnp.dot(acat[xx], high, preferred_element_type=F32)
            total = total + (
                both[0:tok] + both[tok:2 * tok]
                + jnp.dot(acat[xx, 0:tok, :], low, preferred_element_type=F32)
            )
        out_ref[:, cols] = total
        return carry

    lax.fori_loop(0, out_ref.shape[1] // TILE, tile, 0)

    for copy in sends:
        copy.wait_send()

    def sent(k, carry):
        peer = lax.rem(z + k, nz)
        dev = at(y, peer, c)
        rc(ps.at[peer], r1.at[z], p1_s.at[k], p1_r.at[k], dev).wait_send()
        rc(pt, rt1.at[z], pt_s.at[k], pt_r.at[k], dev).wait_send()
        rc(s2.at[peer], r2.at[z], p2_s.at[k], p2_r.at[k], dev).wait_send()
        return carry

    lax.fori_loop(1, nz, sent, 0)


def solution(mesh):
    nz, nx = mesh.shape["seq"] // (2 * NY), mesh.shape["tp"]

    def shards(queries, keys, values, out_weight):
        tok = queries.shape[0]
        depth, columns = out_weight.shape
        part = (nz, 2 * DH // nz, DH)
        dma = pltpu.SemaphoreType.DMA
        vmem = pl.BlockSpec(memory_space=pltpu.VMEM)
        return pl.pallas_call(
            functools.partial(kernel, nz, nx),
            out_shape=jax.ShapeDtypeStruct((tok, columns), F32),
            in_specs=[pl.BlockSpec(memory_space=pltpu.HBM)] * 4,
            out_specs=vmem,
            scratch_shapes=[
                pltpu.VMEM((NY, nz, 2, depth, columns), F32),
                pltpu.VMEM((tok, 4 * DH), F32),
                pltpu.VMEM((tok, 4 * DH), F32),
                pltpu.VMEM((tok, 4 * DH), F32),
                pltpu.VMEM((2,) + part, F32),
                pltpu.VMEM((2, 8, DH), F32),
                pltpu.VMEM(part, F32),
                pltpu.VMEM((8, DH), F32),
                pltpu.VMEM(part, F32),
                pltpu.VMEM((2, DH), F32),
                pltpu.VMEM(part, F32),
                pltpu.VMEM((nz, 2, DH), F32),
                pltpu.VMEM((part[1] + 8, DH), F32),
                pltpu.VMEM((NY, part[1] + 8, DH), F32),
                pltpu.VMEM(part, F32),
                pltpu.VMEM(part, F32),
                pltpu.VMEM(part, F32),
                pltpu.VMEM((2,) + part, F32),
                pltpu.VMEM((8, DH), F32),
                pltpu.VMEM((2, 8, DH), F32),
                pltpu.VMEM((4, tok, DH), F32),
                pltpu.VMEM((4, tok, DH), BF16),
                pltpu.VMEM((4, tok, DH), BF16),
                pltpu.VMEM((4, tok, DH), F32),
                pltpu.VMEM((4, tok, DH), F32),
                pltpu.VMEM((nx, 4, tok, DH), F32),
                pltpu.VMEM((nx, 2 * tok, 4 * DH), BF16),
                dma((4,)),
                pltpu.SemaphoreType.REGULAR((nz // 2 + 1,)),
                pltpu.SemaphoreType.REGULAR((nz // 2 + 1,)),
            ]
            + [dma((nz // 2,))] * 4
            + [dma((nz,))] * 6
            + [dma((NY, nz))] * 2
            + [dma((4,))] * 2
            + [dma((nz,))] * 4
            + [dma((NY,))] * 2
            + [dma((nz,))] * 2
            + [dma((4,))] * 8,
            compiler_params=pltpu.CompilerParams(
                collective_id=0, has_side_effects=True, vmem_limit_bytes=67043328
            ),
        )(queries, keys, values, out_weight)

    return jax.shard_map(
        shards,
        mesh=mesh,
        in_specs=(P("seq", "tp"),) * 4,
        out_specs=P("seq", "tp"),
        check_vma=False,
    )
```

```python
import functools

import jax
import jax.numpy as jnp
from jax import lax
from jax.experimental import pallas as pl
from jax.experimental.pallas import tpu as pltpu
from jax.sharding import PartitionSpec as P

MESH = pl.DeviceIdType.MESH
F32 = jnp.float32
BF16 = jnp.bfloat16
DH = 128
NY = 4
TILE = 256


def phi(a):
    return jnp.where(a > 0, a + 1.0, jnp.exp(jnp.minimum(a, 0.0)))


def rc(src, dst, send_sem, recv_sem, dev):
    return pltpu.make_async_remote_copy(
        src_ref=src, dst_ref=dst, send_sem=send_sem, recv_sem=recv_sem,
        device_id=dev, device_id_type=MESH,
    )


def halves(a):
    high = a.astype(BF16)
    return high, (a - high.astype(F32)).astype(BF16)


def dot3(a, b, dims):
    (ah, al), (bh, bl) = a, b

    def one(p, r):
        return lax.dot_general(p, r, (dims, ((), ())), preferred_element_type=F32)

    return one(ah, bh) + (one(al, bh) + one(ah, bl))


def kernel(
    nz, nx, q_hbm, k_hbm, v_hbm, w_hbm, out_ref,
    w_all, q_ref, k_ref, v_ref, st, tst, sx, tsx, ps, pt, r1, rt1, yt, yr, s2, r2, fs, full,
    ft, ftot, phiq, qh, ql, numl, denl, att, acat,
    in_s, tok_r, tok_l,
    zr_s, zr_r, zl_s, zl_r, yp_s, yp_r, ym_s, ym_r, fd_s, fd_r, sb_s, sb_r,
    e_s, e_r, p1_s, p1_r, pt_s, pt_r, yx_s, yx_r, p2_s, p2_r,
    xr_s, xr_r, xl_s, xl_r, gr_s, gr_r, gl_s, gl_r,
):
    s, x = lax.axis_index("seq"), lax.axis_index("tp")
    c = lax.rem(s, 2)
    z = lax.rem(s // 2, nz)
    y = s // (2 * nz)
    tok = q_ref.shape[0]
    rows = 2 * DH // nz

    def at(yy, zz, cc):
        return {"seq": (yy * nz + zz) * 2 + cc}

    def dz(k):
        return lax.rem(z + (k + nz), nz)

    def dy(k):
        return lax.rem(y + (k + NY), NY)

    sib = at(y, z, 1 - c)
    right, left = {"tp": lax.rem(x + 1, nx)}, {"tp": lax.rem(x + nx - 1, nx)}
    up, down = at(y, dz(1), c), at(y, dz(-1), c)
    up2, down2 = at(y, dz(2), c), at(y, dz(-2), c)
    half = nz // 2

    barrier = pltpu.get_barrier_semaphore()
    near = [sib, right, left, up, down, up2, down2] + [at(dy(k), z, c) for k in range(1, NY)]
    for dev in near:
        pl.semaphore_signal(barrier, inc=1, device_id=dev, device_id_type=MESH)
    inputs = [
        pltpu.make_async_copy(src, dst, in_s.at[i])
        for i, (src, dst) in enumerate(
            ((w_hbm, w_all.at[y, z, c]), (k_hbm, k_ref), (v_hbm, v_ref), (q_hbm, q_ref))
        )
    ]
    for copy in inputs:
        copy.start()
    pl.semaphore_wait(barrier, len(near))

    def token(j):
        if j > 1:
            pl.semaphore_wait(tok_l.at[j - 1], 1)
            pl.semaphore_wait(tok_r.at[j - 1], 1)
        if 2 * j < half:
            pl.semaphore_signal(tok_l.at[j], inc=1, device_id=down2, device_id_type=MESH)
            pl.semaphore_signal(tok_r.at[j], inc=1, device_id=up2, device_id_type=MESH)

    sends = []

    def go(copy):
        copy.start()
        sends.append(copy)

    def zof(m):
        return z if m == 0 else (dz(-m) if m <= half else dz(m - half))

    def slot(yy, m, cc):
        return w_all.at[yy, zof(m), cc]

    def to_sib(k, m):
        ref = slot(dy(-k), m, c)
        go(rc(ref, ref, sb_s.at[k, m], sb_r.at[k, m], sib))

    def have(m):
        src = dst = slot(y, m, c)
        go(rc(src, dst, yp_s.at[m], yp_r.at[m], at(dy(1), z, c)))
        go(rc(src, dst, ym_s.at[m], ym_r.at[m], at(dy(-1), z, c)))
        go(rc(src, dst, sb_s.at[0, m], sb_r.at[0, m], sib))

    def pass_on(m, d):
        ref = slot(y, m, c)
        if m <= half:
            if d + 2 <= half:
                go(rc(ref, ref, zr_s.at[d + 1], zr_r.at[d + 1], up2))
            if d + 1 <= half:
                go(rc(ref, ref, zr_s.at[d], zr_r.at[d], up))
        else:
            if d + 2 < half:
                go(rc(ref, ref, zl_s.at[d + 1], zl_r.at[d + 1], down2))
            if d + 1 < half:
                go(rc(ref, ref, zl_s.at[d], zl_r.at[d], down))

    def z_round(r):
        if r == 0:
            ref = slot(y, 0, c)
            go(rc(ref, ref, zr_s.at[1], zr_r.at[1], up2))
            go(rc(ref, ref, zl_s.at[1], zl_r.at[1], down2))
            go(rc(ref, ref, zr_s.at[0], zr_r.at[0], up))
            go(rc(ref, ref, zl_s.at[0], zl_r.at[0], down))
            have(0)
            return
        for d in (2 * r, 2 * r - 1):
            ref = slot(y, d, c)
            rc(ref, ref, zr_s.at[d - 1], zr_r.at[d - 1], up).wait_recv()
            if d == 2 * r:
                pass_on(d, d)
            if d < half:
                ref = slot(y, half + d, c)
                rc(ref, ref, zl_s.at[d - 1], zl_r.at[d - 1], down).wait_recv()
                if d == 2 * r:
                    pass_on(half + d, d)
        if r not in (3,):
            spread(r)

    def spread(r):
        for d in (2 * r - 1, 2 * r):
            have(d)
            if d < half:
                have(half + d)

    late = []

    def push(k, m):
        late.append((k, m))

    def flush():
        for k, m in late:
            to_sib(k, m)
        late.clear()

    def y_stage(r):
        for m in ((r,) if r in (0, half) else (r, half + r)):
            below, above = slot(dy(-1), m, c), slot(dy(1), m, c)
            rc(below, below, yp_s.at[m], yp_r.at[m], at(dy(1), z, c)).wait_recv()
            if m < half:
                go(rc(below, below, fd_s.at[m], fd_r.at[m], at(dy(1), z, c)))
            push(1, m)
            rc(above, above, ym_s.at[m], ym_r.at[m], at(dy(-1), z, c)).wait_recv()
            if m >= half:
                go(rc(above, above, fd_s.at[m], fd_r.at[m], at(dy(-1), z, c)))
            push(3, m)

    def far_stage(m):
        ref = slot(dy(2), m, c)
        rc(ref, ref, fd_s.at[m], fd_r.at[m], at(dy(1), z, c)).wait_recv()
        to_sib(2, m)

    token(1)
    inputs[0].wait()
    z_round(0)
    inputs[1].wait()
    inputs[2].wait()
    row8 = lax.broadcasted_iota(jnp.int32, (8, DH), 0)
    per = nz // 2
    hops = ((2,), (3,), (4,), ())
    for t in range(4):
        b, hh = (1 - c if t < 2 else c), t % 2
        cols = pl.ds(pl.multiple_of((2 * b + hh) * DH, DH), DH)
        pk = phi(k_ref[:, cols])
        state = dot3(halves(pk), halves(v_ref[:, cols]), ((0,), (0,)))
        st[b, hh * per:(hh + 1) * per] = state.reshape(per, rows, DH)
        total = jnp.broadcast_to(jnp.sum(pk, axis=0, keepdims=True), (8, DH))
        if hh == 0:
            totals = total
        else:
            tst[b] = jnp.where(row8 == 0, totals, total)
        if t == 1:
            go(rc(st.at[b], sx, e_s.at[0], e_r.at[0], sib))
            go(rc(tst.at[b], tsx, e_s.at[1], e_r.at[1], sib))
        for r in hops[t]:
            token(r)
        if t == 1:
            z_round(1)
    rc(st.at[1 - c], sx, e_s.at[0], e_r.at[0], sib).wait_recv()
    rc(tst.at[1 - c], tsx, e_s.at[1], e_r.at[1], sib).wait_recv()
    ps[...] = st[c] + sx[...]
    pt[...] = tst[c, 0:2] + tsx[0:2]

    def send1(k, carry):
        peer = lax.rem(z + k, nz)
        rc(ps.at[peer], r1.at[z], p1_s.at[k], p1_r.at[k], at(y, peer, c)).start()
        rc(pt, rt1.at[z], pt_s.at[k], pt_r.at[k], at(y, peer, c)).start()
        return carry

    lax.fori_loop(1, nz, send1, 0)
    r1[z] = ps[z]
    rt1[z] = pt[...]
    yr[y] = jnp.zeros((rows + 8, DH), F32)

    inputs[3].wait()
    causal = lax.broadcasted_iota(jnp.int32, (tok, tok), 0) >= lax.broadcasted_iota(
        jnp.int32, (tok, tok), 1
    )
    for h in range(4):
        cols = slice(h * DH, (h + 1) * DH)
        pq = phi(q_ref[:, cols])
        parts = halves(pq)
        scores = dot3(parts, halves(phi(k_ref[:, cols])), ((1,), (1,)))
        scores = jnp.where(causal, scores, 0.0)
        phiq[h] = pq
        qh[h], ql[h] = parts
        numl[h] = dot3(halves(scores), halves(v_ref[:, cols]), ((1,), (0,)))
        denl[h] = jnp.broadcast_to(jnp.sum(scores, axis=1, keepdims=True), (tok, DH))

    z_round(2)

    def wait1(k, carry):
        origin = lax.rem(z + nz - k, nz)
        rc(ps.at[0], r1.at[origin], p1_s.at[k], p1_r.at[k], at(y, origin, c)).wait_recv()
        rc(pt, rt1.at[origin], pt_s.at[k], pt_r.at[k], at(y, origin, c)).wait_recv()
        return carry

    lax.fori_loop(1, nz, wait1, 0)
    acc = jnp.zeros((rows, DH), F32)
    acct = jnp.zeros((2, DH), F32)
    mine = jnp.zeros((2, DH), F32)
    for i in range(nz):
        s2[i] = acc
        acc = acc + r1[i]
        mine = mine + jnp.where(i < z, rt1[i], 0.0)
        acct = acct + rt1[i]
    yt[0:rows, :] = acc
    yt[rows:rows + 2, :] = acct
    yt[rows + 2:rows + 8, :] = jnp.zeros((6, DH), F32)
    for k in range(1, NY):
        go(rc(yt, yr.at[y], yx_s.at[k], yx_r.at[k], at(dy(k), z, c)))
    z_round(3)
    spread(3)
    y_stage(0)
    for k in range(1, NY):
        rc(yt, yr.at[dy(-k)], yx_s.at[k], yx_r.at[k], at(dy(k), z, c)).wait_recv()
    base = jnp.zeros((rows + 8, DH), F32)
    for yy in range(NY):
        base = base + jnp.where(yy < y, yr[yy], 0.0)
    for i in range(nz):
        s2[i] = s2[i] + base[0:rows]

    def send2(k, carry):
        peer = lax.rem(z + k, nz)
        rc(s2.at[peer], r2.at[z], p2_s.at[k], p2_r.at[k], at(y, peer, c)).start()
        return carry

    lax.fori_loop(1, nz, send2, 0)
    r2[z] = s2[z]

    mine = mine + base[rows:rows + 2]
    ft[...] = jnp.zeros_like(ft)
    ft[0:2, :] = mine + jnp.where(c == 0, tst[c, 0:2], 0.0)
    go(rc(ft, ftot.at[c], e_s.at[2], e_r.at[2], sib))
    ftot[c, 0:2, :] = mine + jnp.where(c == 1, tsx[0:2], 0.0)
    z_round(4)
    rc(ft, ftot.at[1 - c], e_s.at[2], e_r.at[2], sib).wait_recv()
    for h in range(4):
        total = ftot[h // 2, h % 2:h % 2 + 1, :]
        denl[h] = denl[h] + jnp.sum(phiq[h] * total, axis=1, keepdims=True)

    for r in range(1, 5):
        y_stage(r)

    def wait2(k, carry):
        origin = lax.rem(z + nz - k, nz)
        rc(s2.at[0], r2.at[origin], p2_s.at[k], p2_r.at[k], at(y, origin, c)).wait_recv()
        return carry

    lax.fori_loop(1, nz, wait2, 0)
    fs[...] = r2[...] + jnp.where(c == 0, st[c], 0.0)
    go(rc(fs, full.at[c], e_s.at[3], e_r.at[3], sib))
    full[c] = r2[...] + jnp.where(c == 1, sx[...], 0.0)

    for t in range(4):
        h, hh = lax.rem(2 * c + t, 4), t % 2
        b = c if t < 2 else 1 - c
        if t == 2:
            rc(fs, full.at[1 - c], e_s.at[3], e_r.at[3], sib).wait_recv()
        prior = halves(full[b, hh * per:(hh + 1) * per].reshape(DH, DH))
        num = numl[h] + dot3((qh[h], ql[h]), prior, ((1,), (0,)))
        att[x, h] = num / denl[h]
        go(rc(att.at[x, h], att.at[x, h], xr_s.at[t], xr_r.at[t], right))
        go(rc(att.at[x, h], att.at[x, h], xl_s.at[t], xl_r.at[t], left))

    flush()
    y_stage(5)
    y_stage(6)
    flush()
    xl, xr, xf = lax.rem(x + nx - 1, nx), lax.rem(x + 1, nx), lax.rem(x + 2, nx)
    for t in range(4):
        h = lax.rem(2 * c + t, 4)
        ref = att.at[xl, h]
        rc(ref, ref, xr_s.at[t], xr_r.at[t], right).wait_recv()
        if t % 2 == 0:
            go(rc(ref, ref, gr_s.at[t], gr_r.at[t], right))
        ref = att.at[xr, h]
        rc(ref, ref, xl_s.at[t], xl_r.at[t], left).wait_recv()
        if t % 2 == 1:
            go(rc(ref, ref, gl_s.at[t], gl_r.at[t], left))
        if t % 2 == 1:
            y_stage(7 + t // 2)
            flush()

    for m in [0] + [m for r in range(1, half) for m in (half + r, r)] + [half]:
        far_stage(m)
    for t in range(4):
        h = lax.rem(2 * c + t, 4)
        ref = att.at[xf, h]
        if t % 2 == 0:
            rc(ref, ref, gr_s.at[t], gr_r.at[t], right).wait_recv()
        else:
            rc(ref, ref, gl_s.at[t], gl_r.at[t], left).wait_recv()
    for k in range(NY):
        for m in range(nz):
            ref = slot(dy(-k), m, 1 - c)
            rc(ref, ref, sb_s.at[k, m], sb_r.at[k, m], sib).wait_recv()

    for xx in range(nx):
        for h in range(4):
            high, low = halves(att[xx, h])
            acat[xx, 0:tok, h * DH:(h + 1) * DH] = high
            acat[xx, tok:2 * tok, h * DH:(h + 1) * DH] = low

    def tile(n, carry):
        cols = pl.ds(pl.multiple_of(n * TILE, TILE), TILE)
        total = jnp.zeros((tok, TILE), F32)
        for xx in range(nx):
            wt = w_all[xx, :, :, :, cols].reshape(4 * DH, TILE)
            high, low = halves(wt)
            both = jnp.dot(acat[xx], high, preferred_element_type=F32)
            total = total + (
                both[0:tok] + both[tok:2 * tok]
                + jnp.dot(acat[xx, 0:tok, :], low, preferred_element_type=F32)
            )
        out_ref[:, cols] = total
        return carry

    lax.fori_loop(0, out_ref.shape[1] // TILE, tile, 0)

    for copy in sends:
        copy.wait_send()

    def sent(k, carry):
        peer = lax.rem(z + k, nz)
        dev = at(y, peer, c)
        rc(ps.at[peer], r1.at[z], p1_s.at[k], p1_r.at[k], dev).wait_send()
        rc(pt, rt1.at[z], pt_s.at[k], pt_r.at[k], dev).wait_send()
        rc(s2.at[peer], r2.at[z], p2_s.at[k], p2_r.at[k], dev).wait_send()
        return carry

    lax.fori_loop(1, nz, sent, 0)


def solution(mesh):
    nz, nx = mesh.shape["seq"] // (2 * NY), mesh.shape["tp"]

    def shards(queries, keys, values, out_weight):
        tok = queries.shape[0]
        depth, columns = out_weight.shape
        part = (nz, 2 * DH // nz, DH)
        dma = pltpu.SemaphoreType.DMA
        vmem = pl.BlockSpec(memory_space=pltpu.VMEM)
        return pl.pallas_call(
            functools.partial(kernel, nz, nx),
            out_shape=jax.ShapeDtypeStruct((tok, columns), F32),
            in_specs=[pl.BlockSpec(memory_space=pltpu.HBM)] * 4,
            out_specs=vmem,
            scratch_shapes=[
                pltpu.VMEM((NY, nz, 2, depth, columns), F32),
                pltpu.VMEM((tok, 4 * DH), F32),
                pltpu.VMEM((tok, 4 * DH), F32),
                pltpu.VMEM((tok, 4 * DH), F32),
                pltpu.VMEM((2,) + part, F32),
                pltpu.VMEM((2, 8, DH), F32),
                pltpu.VMEM(part, F32),
                pltpu.VMEM((8, DH), F32),
                pltpu.VMEM(part, F32),
                pltpu.VMEM((2, DH), F32),
                pltpu.VMEM(part, F32),
                pltpu.VMEM((nz, 2, DH), F32),
                pltpu.VMEM((part[1] + 8, DH), F32),
                pltpu.VMEM((NY, part[1] + 8, DH), F32),
                pltpu.VMEM(part, F32),
                pltpu.VMEM(part, F32),
                pltpu.VMEM(part, F32),
                pltpu.VMEM((2,) + part, F32),
                pltpu.VMEM((8, DH), F32),
                pltpu.VMEM((2, 8, DH), F32),
                pltpu.VMEM((4, tok, DH), F32),
                pltpu.VMEM((4, tok, DH), BF16),
                pltpu.VMEM((4, tok, DH), BF16),
                pltpu.VMEM((4, tok, DH), F32),
                pltpu.VMEM((4, tok, DH), F32),
                pltpu.VMEM((nx, 4, tok, DH), F32),
                pltpu.VMEM((nx, 2 * tok, 4 * DH), BF16),
                dma((4,)),
                pltpu.SemaphoreType.REGULAR((nz // 2 + 1,)),
                pltpu.SemaphoreType.REGULAR((nz // 2 + 1,)),
            ]
            + [dma((nz // 2,))] * 4
            + [dma((nz,))] * 6
            + [dma((NY, nz))] * 2
            + [dma((4,))] * 2
            + [dma((nz,))] * 4
            + [dma((NY,))] * 2
            + [dma((nz,))] * 2
            + [dma((4,))] * 8,
            compiler_params=pltpu.CompilerParams(
                collective_id=0, has_side_effects=True, vmem_limit_bytes=67043328
            ),
        )(queries, keys, values, out_weight)

    return jax.shard_map(
        shards,
        mesh=mesh,
        in_specs=(P("seq", "tp"),) * 4,
        out_specs=P("seq", "tp"),
        check_vma=False,
    )
```
